32 devices in a mesh: gz: 16 (over z, x, core), ph: 2 (over y).
Axes of the slice: x: 2, y: 2, z: 4, core: 2. Of those that a mesh axis runs over, the one named last changes fastest.
Arguments:
- frac: bfloat16 [2, 128, 64, 256], P('ph', 'gz'), may hold values from 0.0099487305 to 0.099609375
- velocity: bfloat16 [2, 3, 128, 64, 256], P('ph', None, 'gz'), may hold values from -6 to 6
- gas_vel: bfloat16 [3, 128, 64, 256], P(None, 'gz'), may hold values from -6 to 6
- diameters: float32 [32], replicated, may hold values from 0.5 to 4
- phase_map: int32 [2], P('ph'), may hold values from 0 to 31
- wall_mask: int32 [64, 256], replicated, may hold values 0 or 1
- offsets: int32 [128], replicated, may hold values from 0 to 255
Outputs:
- pressure: float32 [128, 64, 256], P('gz')
- corrected: bfloat16 [2, 3, 128, 64, 256], P('ph', None, 'gz')
The draws below stay inside these ranges and needn't reach their ends.
Inputs may be any that keep to these rules, and one draw needn't show every extreme that they name: `wall_mask`: 1 marks a fluid cell, 0 a lifter or wall cell.
All inputs are finite; a program needn't handle non-finite values.
Results may differ from the reference program's by a relative error of at most 0.001.
Values sent between devices are 32-bit elements; how exact they have to be, the bound alone decides.
A program may use at most 64 MiB of HBM per device.

```python
import math
import jax
import jax.numpy as jnp
from jax import lax

NR = 64
NTH = 256
CLASSES = 32
NZ = 128
PHASES = 2


def draw_gas_vel(key, part):
    base = jax.random.normal(key, (3, NZ, NR, NTH), jnp.float32)
    return jnp.clip(base, -6.0, 6.0).astype(jnp.bfloat16)


def set_ends(result, stream_key, least, high):
    spot = [jax.random.randint(jax.random.fold_in(stream_key, axis), (), 0, length) for axis, length in enumerate(result.shape)]
    longest = result.shape.index(max(result.shape))
    beside = spot[:longest] + [(spot[longest] + 1) % result.shape[longest]] + spot[longest + 1:]
    return result.at[tuple(spot)].set(least).at[tuple(beside)].set(high)


def block_scale(key, shape, pieces, smallest, top_value):
    loudness, own = 1.0, jax.random.fold_in(key, 6)
    for dim, blocks in pieces:
        heights = jnp.exp(jax.random.uniform(jax.random.fold_in(own, dim), (blocks,), jnp.float32, smallest / len(pieces), top_value / len(pieces)))
        loudness = loudness * jnp.repeat(heights, shape[dim] // blocks).reshape([-1 if axis == dim else 1 for axis in range(len(shape))])
    return loudness


def bell_draw(own_key, dims, spread, limit, split=(), held_as=jnp.bfloat16):
    loudness = block_scale(own_key, dims, split, -0.22, 0.18) if split else 1.0
    result = jax.random.normal(own_key, dims, jnp.float32) * spread * loudness
    return jnp.minimum(jnp.maximum(result, -limit), limit).astype(held_as)


def setup_inputs(seed: int = 0) -> dict:
    arg_keys = jax.random.split(jax.random.key(seed), 8)
    return {
        "frac": jnp.clip(jnp.exp(math.log(0.099609375) - 2.3038113 * jax.random.uniform(arg_keys[0], (PHASES, NZ, NR, NTH), jnp.float32) ** block_scale(arg_keys[0], (PHASES, NZ, NR, NTH), ((0, 2), (1, 16)), -0.2, 0.2)), 0.0099487305, 0.099609375).astype(jnp.bfloat16),
        "velocity": bell_draw(arg_keys[1], (PHASES, 3, NZ, NR, NTH), 1.0, 6.0, ((0, 2), (2, 16))),
        "gas_vel": draw_gas_vel(jax.random.fold_in(arg_keys[7], 71), 0),
        "diameters": jnp.clip(jnp.exp(jax.random.uniform(arg_keys[3], (CLASSES,), jnp.float32, math.log(0.5), math.log(4.0))), 0.5, 4.0),
        "phase_map": jax.random.randint(arg_keys[4], (PHASES,), 0, CLASSES).astype(jnp.int32),
        "wall_mask": set_ends((jax.random.randint(arg_keys[5], (NR, NTH), 0, 4) < 3).astype(jnp.int32), jax.random.fold_in(arg_keys[5], 1), 0, 1),
        "offsets": set_ends(jax.random.randint(arg_keys[6], (NZ,), 0, NTH), jax.random.fold_in(arg_keys[6], 1), 0, NTH - 1).astype(jnp.int32),
    }


DT_STEP = 0.5
DRAG_SCALE = 20.0
COMPRESS = 0.005

def phase_terms(slot, frac, velocity, gas, diameters, phase_map):
    which = (jnp.arange(CLASSES, dtype=jnp.int32) == phase_map[slot]).astype(jnp.float32)
    size_here = jnp.sum(diameters * which)
    volume = frac[slot].astype(jnp.float32)
    slip = velocity[slot].astype(jnp.float32) - gas
    speed = jnp.sqrt(1.0 + lax.optimization_barrier(jnp.sum(slip * slip, 0)))
    beta = DRAG_SCALE * volume / (size_here * size_here) * (1.0 + 0.15 * speed)
    relax = 1.0 / (1.0 + DT_STEP * beta)
    return (volume, relax, slip)

def eigen_fft(count):
    wave = jnp.arange(count, dtype=jnp.float32)
    return 2.0 - 2.0 * jnp.cos(2.0 * math.pi / count * wave)

def reference(frac, velocity, gas_vel, diameters, phase_map, wall_mask, offsets):
    angle_step = 2.0 * math.pi / NTH
    around_idx = (jnp.arange(NTH, dtype=jnp.int32)[None, :] - offsets[:, None]) % NTH
    fluid = jnp.transpose(jnp.take(wall_mask, around_idx, axis=1), (1, 0, 2)).astype(jnp.float32)
    open_radial = fluid * jnp.concatenate([fluid[:, 1:], jnp.zeros_like(fluid[:, :1])], 1)
    open_around = fluid * jnp.roll(fluid, -1, 2)
    open_axial = fluid * jnp.roll(fluid, -1, 0)
    radii = (jnp.arange(NR, dtype=jnp.float32) + 0.5)[:, None]
    gas = gas_vel.astype(jnp.float32)
    total = gas
    for slot in range(PHASES):
        volume, relax, slip = phase_terms(slot, frac, velocity, gas, diameters, phase_map)
        total = total + volume * relax * slip
    flux_radial = total[0] * open_radial
    flux_around = total[1] * open_around
    flux_axial = total[2] * open_axial
    radial_prev = jnp.concatenate([jnp.zeros_like(flux_radial[:, :1]), flux_radial[:, :-1]], 1)
    source = ((radii + 0.5) * flux_radial - (radii - 0.5) * radial_prev) / radii
    source = source + (flux_around - jnp.roll(flux_around, 1, 2)) / (radii * angle_step)
    source = (source + flux_axial - jnp.roll(flux_axial, 1, 0)) / DT_STEP
    hat = jnp.fft.fft(jnp.fft.fft(source, axis=0), axis=2)
    stacked = jnp.stack([jnp.real(hat), jnp.imag(hat)], -1)
    right = -jnp.transpose(stacked, (0, 2, 1, 3))
    radius_vec = jnp.arange(NR, dtype=jnp.float32) + 0.5
    inner = radius_vec - 0.5
    outer = jnp.where(jnp.arange(NR) == NR - 1, 0.0, radius_vec + 0.5).astype(radius_vec.dtype)
    diag = COMPRESS + eigen_fft(NZ)[:, None, None] + eigen_fft(NTH)[None, :, None] / (radius_vec * angle_step) ** 2 + ((outer + inner) / radius_vec)[None, None, :]
    lower = jnp.broadcast_to(-inner / radius_vec, diag.shape)
    upper = jnp.broadcast_to(-outer / radius_vec, diag.shape)
    solved = jnp.stack([lax.linalg.tridiagonal_solve(lower, diag, upper, right[..., j:j + 1])[..., 0] for j in range(2)], -1)
    solved = jnp.transpose(solved, (0, 2, 1, 3))
    spectrum = lax.complex(solved[..., 0], solved[..., 1])
    pressure = jnp.real(jnp.fft.ifft(jnp.fft.ifft(spectrum, axis=0), axis=2)).astype(jnp.float32)
    radial_step = (jnp.concatenate([pressure[:, 1:], pressure[:, -1:]], 1) - pressure) * open_radial
    around_step = (jnp.roll(pressure, -1, 2) - pressure) / (radii * angle_step) * open_around
    axial_step = (jnp.roll(pressure, -1, 0) - pressure) * open_axial
    gradient = jnp.stack([radial_step, around_step, axial_step])
    results = []
    for slot in range(PHASES):
        volume, relax, slip = phase_terms(slot, frac, velocity, gas, diameters, phase_map)
        results.append((gas + relax * slip - DT_STEP * gradient).astype(jnp.bfloat16))
    return (pressure, jnp.stack(results))
```

```python
import functools
import math

import jax
import jax.numpy as jnp
import numpy as np
from jax import lax
from jax.experimental import pallas as pl
from jax.experimental.pallas import tpu as pltpu
from jax.sharding import PartitionSpec as P

DT_STEP = 0.5
DRAG_SCALE = 20.0
COMPRESS = 0.005
HIGHEST = lax.Precision.HIGHEST


def from_behind(block, axis, distance):
    devices = range(lax.axis_size(axis))
    route = [((i - distance) % len(devices), i) for i in devices]
    return lax.ppermute(block, axis, route)


def real_basis(count):
    index_rows = jnp.arange(count, dtype=jnp.int32)[:, None]
    column = jnp.arange(count, dtype=jnp.int32)[None, :]
    half = count // 2
    wave = jnp.where(column <= half, column, column - half)
    angle = 2.0 * math.pi / count * (index_rows * wave % count).astype(jnp.float32)
    scaled = math.sqrt(2.0 / count)
    cosine = jnp.cos(angle)
    table = jnp.where(column < half, scaled * cosine, scaled * jnp.sin(angle))
    return jnp.where((column == 0) | (column == half), cosine / math.sqrt(count), table)


def eigen_values(count):
    column = jnp.arange(count, dtype=jnp.int32)
    half = count // 2
    wave = jnp.where(column <= half, column, column - half).astype(jnp.float32)
    return 2.0 - 2.0 * jnp.cos(2.0 * math.pi / count * wave)


def rotate_mask(wall_mask, turns, around_count):
    around_idx = (
        jnp.arange(around_count, dtype=jnp.int32)[None, :] - turns[:, None]
    ) % around_count
    return jnp.transpose(jnp.take(wall_mask, around_idx, axis=1), (1, 0, 2)).astype(jnp.float32)


def radial_solve(spectral, axial_eig, theta_eig, radius_vec, angle_step):
    radial_count = radius_vec.shape[0]
    inner = radius_vec - 0.5
    outer = jnp.where(jnp.arange(radial_count) == radial_count - 1, 0.0, radius_vec + 0.5)
    diag = (
        COMPRESS
        + axial_eig[:, None, None]
        + theta_eig[None, :, None] / (radius_vec * angle_step) ** 2
        + ((outer + inner) / radius_vec)[None, None, :]
    )
    lower = jnp.broadcast_to(-inner / radius_vec, diag.shape)
    upper = jnp.broadcast_to(-outer / radius_vec, diag.shape)
    right = -jnp.transpose(spectral, (0, 2, 1))[..., None]
    solved = lax.linalg.tridiagonal_solve(lower, diag, upper, right)[..., 0]
    return jnp.transpose(solved, (0, 2, 1))


def to_space(modes, around_table):
    return jnp.dot(
        modes.reshape(-1, around_table.shape[0]), around_table.T, precision=HIGHEST
    ).reshape(modes.shape)


def shards(frac, velocity, gas_vel, diameters, phase_map, wall_mask, offsets):
    plane_count = frac.shape[1]
    radial_count = frac.shape[2]
    around_count = frac.shape[3]
    axial_total = offsets.shape[0]
    phase_count = lax.axis_size("ph")
    slab_index = lax.axis_index("gz")
    first_plane = slab_index * plane_count
    angle_step = 2.0 * math.pi / around_count
    plane_ids = (first_plane + jnp.arange(plane_count + 1, dtype=jnp.int32)) % axial_total
    fluid_all = rotate_mask(wall_mask, jnp.take(offsets, plane_ids), around_count)
    fluid = fluid_all[:plane_count]
    open_radial = fluid * jnp.concatenate([fluid[:, 1:], jnp.zeros_like(fluid[:, :1])], 1)
    open_around = fluid * jnp.roll(fluid, -1, 2)
    open_axial = fluid * fluid_all[1:]
    radius_vec = jnp.arange(radial_count, dtype=jnp.float32) + 0.5
    radii = radius_vec[:, None]
    which = (jnp.arange(diameters.shape[0], dtype=jnp.int32) == phase_map[0]).astype(jnp.float32)
    size_here = jnp.sum(diameters * which)
    volume = frac[0].astype(jnp.float32)
    gas = gas_vel.astype(jnp.float32)
    slip = velocity[0].astype(jnp.float32) - gas
    speed = jnp.sqrt(1.0 + jnp.sum(slip * slip, 0))
    beta = DRAG_SCALE * volume / (size_here * size_here) * (1.0 + 0.15 * speed)
    relax = 1.0 / (1.0 + DT_STEP * beta)
    predicted = gas + relax * slip
    share = volume * relax * slip + gas / phase_count
    flux_radial = share[0] * open_radial
    flux_around = share[1] * open_around
    flux_axial = share[2] * open_axial
    below = from_behind(flux_axial[-1:], "gz", 1)
    axial_prev = jnp.concatenate([below, flux_axial[:-1]], 0)
    radial_prev = jnp.concatenate([jnp.zeros_like(flux_radial[:, :1]), flux_radial[:, :-1]], 1)
    term = ((radii + 0.5) * flux_radial - (radii - 0.5) * radial_prev) / radii
    term = term + (flux_around - jnp.roll(flux_around, 1, 2)) / (radii * angle_step)
    term = (term + flux_axial - axial_prev) / DT_STEP
    around_table = real_basis(around_count)
    axial_table = real_basis(axial_total)
    axial_eig = eigen_values(axial_total)
    axial_step = None
    source = lax.psum(term, "ph")
    modes = jnp.dot(source.reshape(-1, around_count), around_table, precision=HIGHEST).reshape(
        source.shape
    )
    pencil = lax.all_to_all(modes, "gz", split_axis=2, concat_axis=0, tiled=True)
    mode_count = pencil.shape[2]
    theta_eig = lax.dynamic_slice_in_dim(
        eigen_values(around_count), slab_index * mode_count, mode_count
    )
    flat = pencil.reshape(axial_total, -1)
    spectral = jnp.dot(axial_table.T, flat, precision=HIGHEST).reshape(pencil.shape)
    solved = radial_solve(spectral, axial_eig, theta_eig, radius_vec, angle_step)
    space = jnp.dot(axial_table, solved.reshape(axial_total, -1), precision=HIGHEST).reshape(
        pencil.shape
    )
    ahead = jnp.roll(space, -1, 0) - space
    back, back_step = (
        lax.all_to_all(space, "gz", split_axis=0, concat_axis=2, tiled=True),
        lax.all_to_all(ahead, "gz", split_axis=0, concat_axis=2, tiled=True),
    )
    pressure = to_space(back, around_table)
    axial_step = to_space(back_step, around_table)
    radial_step = (jnp.concatenate([pressure[:, 1:], pressure[:, -1:]], 1) - pressure) * open_radial
    around_step = (jnp.roll(pressure, -1, 2) - pressure) / (radii * angle_step) * open_around
    gradient = jnp.stack([radial_step, around_step, axial_step * open_axial])
    corrected = (predicted - DT_STEP * gradient).astype(jnp.bfloat16)[None]
    return (pressure, corrected)


MESH_ID = pl.DeviceIdType.MESH


def split_low(x):
    high = x.astype(jnp.bfloat16)
    return high, (x - high.astype(jnp.float32)).astype(jnp.bfloat16)


def triple_dot(x, table_high, table_low):
    high, low = split_low(x)
    out = jnp.dot(high, table_high, preferred_element_type=jnp.float32)
    out = out + jnp.dot(low, table_high, preferred_element_type=jnp.float32)
    return out + jnp.dot(high, table_low, preferred_element_type=jnp.float32)


def np_high_low(table):
    high = table.astype(jnp.bfloat16)
    low = (table - high.astype(np.float64)).astype(jnp.bfloat16)
    return high, low


@functools.lru_cache(maxsize=None)
def operator_tables(radial, around, axial, planes):
    half = around // 2
    rows = np.arange(around)[:, None]
    column = np.arange(around)[None, :]
    wave = np.where(column <= half, column, column - half)
    angle = 2.0 * np.pi / around * (rows * wave % around)
    basis = np.sqrt(2.0 / around) * np.where(column <= half, np.cos(angle), np.sin(angle))
    basis = np.where((column == 0) | (column == half), np.cos(angle) / np.sqrt(around), basis)
    radius = np.arange(radial) + 0.5
    inner = radius - 0.5
    outer = np.where(np.arange(radial) == radial - 1, 0.0, radius + 0.5)
    step = 2.0 * np.pi / around
    vectors, values = [], []
    for m in range(half + 1):
        eig = 2.0 - 2.0 * np.cos(2.0 * np.pi / around * m)
        matrix = np.diag((outer + inner) / radius + eig / (radius * step) ** 2)
        off = -outer[:-1] / np.sqrt(radius[:-1] * radius[1:])
        matrix = matrix + np.diag(off, 1) + np.diag(off, -1)
        value, vector = np.linalg.eigh(matrix)
        vector = vector * np.where(vector[:1] < 0.0, -1.0, 1.0)
        values.append(value)
        vectors.append(vector)
    vectors = np.stack(vectors, -1)
    values = np.maximum(np.stack(values, -1), 0.0)
    first = vectors[:, :, :half]
    nyquist = np.zeros((radial, max(radial, 128)))
    nyquist[:, :radial] = vectors[:, :, half].T
    other = np.concatenate([values[:, half:], values[:, 1:half]], -1)
    over = COMPRESS + np.stack([values[:, :half], other])
    root = np.sqrt(over * (over + 4.0))
    ratio = 2.0 / (2.0 + over + root)
    jump = ratio**planes
    wrap = 1.0 / (1.0 - ratio**axial)
    line = np.stack([ratio, 1.0 / root, jump, wrap], 1).astype(np.float32)
    ahead = np_high_low(basis)
    back = np_high_low(basis.T.copy())
    return (
        first.astype(np.float32),
        nyquist.astype(np.float32),
        line,
        np.stack(ahead),
        np.stack(back),
    )


def drum_kernel(
    gz_count,
    offsets_ref,
    diameters_ref,
    map_ref,
    frac_ref,
    velocity_ref,
    gas_ref,
    wall_ref,
    nyquist_ref,
    line_ref,
    ahead_ref,
    back_ref,
    radial_hbm,
    pressure_ref,
    corrected_ref,
    fluid,
    pred,
    term,
    axial_flux,
    halo,
    modes,
    partner,
    radial,
    radial_back,
    lines,
    ends_out,
    ends_in,
    states_out,
    states_in,
    solved,
    result,
    space,
    table_sem,
    halo_sem,
    swap_send,
    swap_recv,
    ends_send,
    ends_recv,
    states_send,
    states_recv,
    back_send,
    back_recv,
):
    me = lax.axis_index("gz")
    ph = lax.axis_index("ph")
    other = 1 - ph
    planes, rows, around = term.shape
    half = around // 2
    axial_total = offsets_ref.shape[0]
    blocks = rows // 8
    angle_step = 2.0 * math.pi / around

    barrier = pltpu.get_barrier_semaphore()
    for hop in range(1, gz_count):
        pl.semaphore_signal(
            barrier, inc=1, device_id=(lax.rem(me + hop, gz_count), ph), device_id_type=MESH_ID
        )
    pl.semaphore_signal(barrier, inc=1, device_id=(me, other), device_id_type=MESH_ID)

    table_copy = pltpu.make_async_copy(radial_hbm, radial, table_sem)
    table_copy.start()

    radii = lax.broadcasted_iota(jnp.int32, (rows, around), 0).astype(jnp.float32) + 0.5
    row_id = lax.broadcasted_iota(jnp.int32, (rows, around), 0)
    wall = wall_ref[...].astype(jnp.float32).astype(jnp.bfloat16)
    from_col = lax.broadcasted_iota(jnp.int32, (around, around), 0)
    to_col = lax.broadcasted_iota(jnp.int32, (around, around), 1)
    gap = to_col - from_col

    def rotate(z, carry):
        turn = offsets_ref[lax.rem(me * planes + z, axial_total)]
        hit = (gap == turn) | (gap == turn - around)
        one_hot = jnp.where(hit, 1.0, 0.0).astype(jnp.bfloat16)
        fluid[z] = jnp.dot(wall, one_hot, preferred_element_type=jnp.float32)
        return carry

    lax.fori_loop(0, planes + 1, rotate, 0)

    size = diameters_ref[map_ref[0]]
    axial_flux[0] = jnp.zeros((rows, around), jnp.float32)

    def opens(z):
        here = fluid[z]
        open_radial = jnp.where(row_id == rows - 1, 0.0, here * pltpu.roll(here, rows - 1, 0))
        open_around = here * pltpu.roll(here, around - 1, 1)
        return open_radial, open_around, here * fluid[z + 1]

    weight = -jnp.sqrt(radii) / DT_STEP
    share = 1.0 / lax.axis_size("ph")

    def source(z, carry):
        volume = frac_ref[0, z].astype(jnp.float32)
        gas = [gas_ref[a, z].astype(jnp.float32) for a in range(3)]
        slip = [velocity_ref[0, a, z].astype(jnp.float32) - gas[a] for a in range(3)]
        speed = jnp.sqrt(1.0 + (slip[0] * slip[0] + slip[1] * slip[1] + slip[2] * slip[2]))
        beta = DRAG_SCALE * volume / (size * size) * (1.0 + 0.15 * speed)
        relax = 1.0 / (1.0 + DT_STEP * beta)
        open_radial, open_around, open_axial = opens(z)
        for a in range(3):
            pred[a, z] = gas[a] + relax * slip[a]
        pull = volume * relax
        flux_radial = (pull * slip[0] + share * gas[0]) * open_radial
        flux_around = (pull * slip[1] + share * gas[1]) * open_around
        flux_axial = (pull * slip[2] + share * gas[2]) * open_axial
        axial_flux[z + 1] = flux_axial
        out = (radii + 0.5) * flux_radial
        inward = jnp.where(row_id == 0, 0.0, pltpu.roll(out, 1, 0))
        total = (out - inward) / radii
        total = total + (flux_around - pltpu.roll(flux_around, 1, 1)) / (radii * angle_step)
        term[z] = (total + flux_axial - axial_flux[z]) * weight
        return carry

    lax.fori_loop(0, planes, source, 0)

    pl.semaphore_wait(barrier, gz_count)

    halo_copy = pltpu.make_async_remote_copy(
        src_ref=axial_flux.at[planes],
        dst_ref=halo,
        send_sem=halo_sem.at[0],
        recv_sem=halo_sem.at[1],
        device_id=(lax.rem(me + 1, gz_count), ph),
        device_id_type=MESH_ID,
    )
    halo_copy.start()

    def swap(z):
        return pltpu.make_async_remote_copy(
            src_ref=modes.at[other, z],
            dst_ref=partner.at[z],
            send_sem=swap_send.at[z],
            recv_sem=swap_recv.at[z],
            device_id=(me, other),
            device_id_type=MESH_ID,
        )

    def to_modes(z, value):
        out = triple_dot(value, ahead_ref[0], ahead_ref[1])
        modes[0, z] = out[:, :half]
        modes[1, z] = out[:, half:]
        swap(z).start()

    def send_modes(k, carry):
        to_modes(k, term[k])
        return carry

    lax.fori_loop(1, planes, send_modes, 0)
    halo_copy.wait()
    to_modes(0, term[0] - halo[...] * weight)

    table_copy.wait()
    is_other = jnp.where(ph == 1, 1, 0)
    lane0 = (lax.broadcasted_iota(jnp.int32, (rows, half), 1) == 0) & (
        jnp.broadcast_to(is_other, (rows, half)) == 1
    )
    for r in range(rows):
        fill = jnp.broadcast_to(nyquist_ref[:, r : r + 1], (rows, half))
        radial[pl.ds(r * rows, rows), :] = jnp.where(lane0, fill, radial[pl.ds(r * rows, rows), :])

    def apply(table, load, z):
        def add(k, acc):
            for j in range(8):
                r = k * 8 + j
                line = jnp.broadcast_to(load(z, r), (rows, half))
                acc = acc + table[pl.ds(pl.multiple_of(r * rows, rows), rows), :] * line
            return acc

        return lax.fori_loop(0, rows // 8, add, jnp.zeros((rows, half), jnp.float32))

    def load_term(z, r):
        return modes[ph, z, pl.ds(r, 1), :] + partner[z, pl.ds(r, 1), :]

    def forward(k, carry):
        z = lax.rem(k + 1, planes)
        swap(z).wait_recv()
        lines[z] = apply(radial, load_term, z)
        return carry

    lax.fori_loop(0, planes, forward, 0)

    ratio = line_ref[ph, 0]
    rising = lines[0]
    for z in range(1, planes):
        rising = rising * ratio + lines[z]
    falling = lines[planes - 1]
    for z in range(planes - 2, -1, -1):
        falling = falling * ratio + lines[z]
    for j in range(blocks):
        ends_out[j] = rising[8 * j : 8 * j + 8]
        ends_out[blocks + j] = falling[8 * j : 8 * j + 8]

    def exchange(src, dst, send, recv, hop, sender):
        to = lax.rem(me + hop, gz_count)
        at = lax.rem(me + gz_count - hop, gz_count) if sender else me
        return pltpu.make_async_remote_copy(
            src_ref=src.at[to],
            dst_ref=dst.at[at],
            send_sem=send.at[hop],
            recv_sem=recv.at[hop],
            device_id=(to, ph),
            device_id_type=MESH_ID,
        )

    for hop in range(1, gz_count):
        exchange(ends_out, ends_in, ends_send, ends_recv, hop, False).start()
    ends_in[me] = ends_out[me]

    def flip(l, carry):
        radial_back[pl.ds(pl.multiple_of(l * rows, rows), rows), :] = radial[
            pl.ds(l, rows, stride=rows), :
        ]
        return carry

    lax.fori_loop(0, rows, flip, 0)

    for hop in range(1, gz_count):
        exchange(ends_out, ends_in, ends_send, ends_recv, hop, True).wait_recv()

    is_rise = 1 - me // blocks
    mine = lax.rem(me, blocks)
    jump = line_ref[ph, 2, pl.ds(pl.multiple_of(mine * 8, 8), 8), :]
    wrap = line_ref[ph, 3, pl.ds(pl.multiple_of(mine * 8, 8), 8), :]
    order = [is_rise * s + (1 - is_rise) * (gz_count - 1 - s) for s in range(gz_count)]
    state = jnp.zeros((8, half), jnp.float32)
    for s in range(gz_count):
        state = state * jump + ends_in[order[s]]
    state = state * wrap
    for s in range(gz_count):
        states_out[order[s]] = state
        state = state * jump + ends_in[order[s]]

    for hop in range(1, gz_count):
        exchange(states_out, states_in, states_send, states_recv, hop, False).start()
    states_in[me] = states_out[me]
    for hop in range(1, gz_count):
        exchange(states_out, states_in, states_send, states_recv, hop, True).wait_recv()

    scale = line_ref[ph, 1]
    right = jnp.concatenate([states_in[blocks + j] for j in range(blocks)], 0)
    left = jnp.concatenate([states_in[j] for j in range(blocks)], 0)
    solved[planes] = right
    behind = right * ratio
    for z in range(planes - 1, -1, -1):
        solved[z] = behind
        behind = (behind + lines[z]) * ratio
    ahead_state = left
    for z in range(planes):
        ahead_state = ahead_state * ratio + lines[z]
        solved[z] = (solved[z] + ahead_state) * scale
    solved[planes] = (solved[planes] + ahead_state * ratio) * scale

    def give(z, index):
        return pltpu.make_async_remote_copy(
            src_ref=result.at[index, z],
            dst_ref=result.at[index, z],
            send_sem=back_send.at[z],
            recv_sem=back_recv.at[z],
            device_id=(me, other),
            device_id_type=MESH_ID,
        )

    def load_solved(z, r):
        return solved[z, pl.ds(r, 1), :]

    shrink = 1.0 / jnp.sqrt(radii[:, :half])

    def inverse(z, carry):
        result[ph, z] = apply(radial_back, load_solved, z) * shrink
        give(z, ph).start()
        return carry

    lax.fori_loop(0, planes + 1, inverse, 0)

    def finish(z, carry):
        give(z, other).wait_recv()
        both = jnp.concatenate([result[0, z], result[1, z]], 1)
        space[z] = triple_dot(both, back_ref[0], back_ref[1])
        return carry

    lax.fori_loop(0, planes + 1, finish, 0)

    def correct(z, carry):
        here = space[z]
        pressure_ref[z] = here
        open_radial, open_around, open_axial = opens(z)
        radial_step = (pltpu.roll(here, rows - 1, 0) - here) * open_radial
        around_step = (pltpu.roll(here, around - 1, 1) - here) / (radii * angle_step) * open_around
        axial_step = (space[z + 1] - here) * open_axial
        for a, step in enumerate((radial_step, around_step, axial_step)):
            corrected_ref[0, a, z] = (pred[a, z] - DT_STEP * step).astype(jnp.bfloat16)
        return carry

    lax.fori_loop(0, planes, correct, 0)

    for z in range(planes):
        swap(z).wait_send()
    for hop in range(1, gz_count):
        exchange(ends_out, ends_in, ends_send, ends_recv, hop, False).wait_send()
        exchange(states_out, states_in, states_send, states_recv, hop, False).wait_send()
    for z in range(planes + 1):
        give(z, ph).wait_send()


def drum_step(gz_count, frac, velocity, gas_vel, diameters, phase_map, wall_mask, offsets):
    planes, rows, around = frac.shape[1:]
    half = around // 2
    first, nyquist, line, ahead, back = operator_tables(rows, around, offsets.shape[0], planes)
    smem = pl.BlockSpec(memory_space=pltpu.SMEM)
    vmem = pl.BlockSpec(memory_space=pltpu.VMEM)
    f32 = jnp.float32
    dma = pltpu.SemaphoreType.DMA
    ends = (gz_count, 8, half)
    return pl.pallas_call(
        functools.partial(drum_kernel, gz_count),
        out_shape=(
            jax.ShapeDtypeStruct((planes, rows, around), f32),
            jax.ShapeDtypeStruct((1, 3, planes, rows, around), jnp.bfloat16),
        ),
        in_specs=[smem] * 3 + [vmem] * 8 + [pl.BlockSpec(memory_space=pl.ANY)],
        out_specs=(vmem, vmem),
        scratch_shapes=[
            pltpu.VMEM((planes + 1, rows, around), f32),
            pltpu.VMEM((3, planes, rows, around), f32),
            pltpu.VMEM((planes, rows, around), f32),
            pltpu.VMEM((planes + 1, rows, around), f32),
            pltpu.VMEM((rows, around), f32),
            pltpu.VMEM((2, planes, rows, half), f32),
            pltpu.VMEM((planes, rows, half), f32),
            pltpu.VMEM((rows * rows, half), f32),
            pltpu.VMEM((rows * rows, half), f32),
            pltpu.VMEM((planes, rows, half), f32),
            pltpu.VMEM(ends, f32),
            pltpu.VMEM(ends, f32),
            pltpu.VMEM(ends, f32),
            pltpu.VMEM(ends, f32),
            pltpu.VMEM((planes + 1, rows, half), f32),
            pltpu.VMEM((2, planes + 1, rows, half), f32),
            pltpu.VMEM((planes + 1, rows, around), f32),
            dma,
            dma((2,)),
            dma((planes,)),
            dma((planes,)),
            dma((gz_count,)),
            dma((gz_count,)),
            dma((gz_count,)),
            dma((gz_count,)),
            dma((planes + 1,)),
            dma((planes + 1,)),
        ],
        compiler_params=pltpu.CompilerParams(
            collective_id=0, has_side_effects=True, vmem_limit_bytes=56 * 1024 * 1024
        ),
    )(
        offsets,
        diameters,
        phase_map,
        frac,
        velocity,
        gas_vel,
        wall_mask,
        jnp.asarray(nyquist),
        jnp.asarray(line),
        jnp.asarray(ahead),
        jnp.asarray(back),
        jnp.asarray(first.reshape(rows * rows, half)),
    )


def solution(mesh):
    in_specs = (
        P("ph", "gz", None, None),
        P("ph", None, "gz", None, None),
        P(None, "gz", None, None),
        P(),
        P("ph"),
        P(),
        P(),
    )
    out_specs = (P("gz", None, None), P("ph", None, "gz", None, None))
    gz_count, ph_count = mesh.shape["gz"], mesh.shape["ph"]

    def body(frac, *rest):
        rows, around = frac.shape[2:]
        fits = ph_count == 2 and around == 256 and rows <= 128
        if fits and rows * 2 == gz_count * 8 and frac.shape[1] <= 8:
            return drum_step(gz_count, frac, *rest)
        return shards(frac, *rest)

    return jax.shard_map(body, mesh=mesh, in_specs=in_specs, out_specs=out_specs, check_vma=False)
```

```python
import functools
import math

import jax
import jax.numpy as jnp
import numpy as np
from jax import lax
from jax.experimental import pallas as pl
from jax.experimental.pallas import tpu as pltpu
from jax.sharding import PartitionSpec as P

DT_STEP = 0.5
DRAG_SCALE = 20.0
COMPRESS = 0.005
CORRECT_STEPS = 2
HIGHEST = lax.Precision.HIGHEST


def from_behind(block, axis, distance):
    devices = range(lax.axis_size(axis))
    route = [((i - distance) % len(devices), i) for i in devices]
    return lax.ppermute(block, axis, route)


def real_basis(count):
    index_rows = jnp.arange(count, dtype=jnp.int32)[:, None]
    column = jnp.arange(count, dtype=jnp.int32)[None, :]
    half = count // 2
    wave = jnp.where(column <= half, column, column - half)
    angle = 2.0 * math.pi / count * (index_rows * wave % count).astype(jnp.float32)
    scaled = math.sqrt(2.0 / count)
    cosine = jnp.cos(angle)
    table = jnp.where(column < half, scaled * cosine, scaled * jnp.sin(angle))
    return jnp.where((column == 0) | (column == half), cosine / math.sqrt(count), table)


def eigen_values(count):
    column = jnp.arange(count, dtype=jnp.int32)
    half = count // 2
    wave = jnp.where(column <= half, column, column - half).astype(jnp.float32)
    return 2.0 - 2.0 * jnp.cos(2.0 * math.pi / count * wave)


def rotate_mask(wall_mask, turns, around_count):
    around_idx = (
        jnp.arange(around_count, dtype=jnp.int32)[None, :] - turns[:, None]
    ) % around_count
    return jnp.transpose(jnp.take(wall_mask, around_idx, axis=1), (1, 0, 2)).astype(jnp.float32)


def radial_solve(spectral, axial_eig, theta_eig, radius_vec, angle_step):
    radial_count = radius_vec.shape[0]
    inner = radius_vec - 0.5
    outer = jnp.where(jnp.arange(radial_count) == radial_count - 1, 0.0, radius_vec + 0.5)
    diag = (
        COMPRESS
        + axial_eig[:, None, None]
        + theta_eig[None, :, None] / (radius_vec * angle_step) ** 2
        + ((outer + inner) / radius_vec)[None, None, :]
    )
    lower = jnp.broadcast_to(-inner / radius_vec, diag.shape)
    upper = jnp.broadcast_to(-outer / radius_vec, diag.shape)
    right = -jnp.transpose(spectral, (0, 2, 1))[..., None]
    solved = lax.linalg.tridiagonal_solve(lower, diag, upper, right)[..., 0]
    return jnp.transpose(solved, (0, 2, 1))


def to_space(modes, around_table):
    return jnp.dot(
        modes.reshape(-1, around_table.shape[0]), around_table.T, precision=HIGHEST
    ).reshape(modes.shape)


def shards(frac, velocity, gas_vel, diameters, phase_map, wall_mask, offsets):
    plane_count = frac.shape[1]
    radial_count = frac.shape[2]
    around_count = frac.shape[3]
    axial_total = offsets.shape[0]
    phase_count = lax.axis_size("ph")
    slab_index = lax.axis_index("gz")
    first_plane = slab_index * plane_count
    angle_step = 2.0 * math.pi / around_count
    plane_ids = (first_plane + jnp.arange(plane_count + 1, dtype=jnp.int32)) % axial_total
    fluid_all = rotate_mask(wall_mask, jnp.take(offsets, plane_ids), around_count)
    fluid = fluid_all[:plane_count]
    open_radial = fluid * jnp.concatenate([fluid[:, 1:], jnp.zeros_like(fluid[:, :1])], 1)
    open_around = fluid * jnp.roll(fluid, -1, 2)
    open_axial = fluid * fluid_all[1:]
    radius_vec = jnp.arange(radial_count, dtype=jnp.float32) + 0.5
    radii = radius_vec[:, None]
    which = (jnp.arange(diameters.shape[0], dtype=jnp.int32) == phase_map[0]).astype(jnp.float32)
    size_here = jnp.sum(diameters * which)
    volume = frac[0].astype(jnp.float32)
    gas = gas_vel.astype(jnp.float32)
    slip = velocity[0].astype(jnp.float32) - gas
    speed = jnp.sqrt(1.0 + jnp.sum(slip * slip, 0))
    beta = DRAG_SCALE * volume / (size_here * size_here) * (1.0 + 0.15 * speed)
    relax = 1.0 / (1.0 + DT_STEP * beta)
    predicted = gas + relax * slip
    share = volume * relax * slip + gas / phase_count
    flux_radial = share[0] * open_radial
    flux_around = share[1] * open_around
    flux_axial = share[2] * open_axial
    below = from_behind(flux_axial[-1:], "gz", 1)
    axial_prev = jnp.concatenate([below, flux_axial[:-1]], 0)
    radial_prev = jnp.concatenate([jnp.zeros_like(flux_radial[:, :1]), flux_radial[:, :-1]], 1)
    term = ((radii + 0.5) * flux_radial - (radii - 0.5) * radial_prev) / radii
    term = term + (flux_around - jnp.roll(flux_around, 1, 2)) / (radii * angle_step)
    term = (term + flux_axial - axial_prev) / DT_STEP
    around_table = real_basis(around_count)
    axial_table = real_basis(axial_total)
    axial_eig = eigen_values(axial_total)
    axial_step = None
    source = lax.psum(term, "ph")
    modes = jnp.dot(source.reshape(-1, around_count), around_table, precision=HIGHEST).reshape(
        source.shape
    )
    pencil = lax.all_to_all(modes, "gz", split_axis=2, concat_axis=0, tiled=True)
    mode_count = pencil.shape[2]
    theta_eig = lax.dynamic_slice_in_dim(
        eigen_values(around_count), slab_index * mode_count, mode_count
    )
    flat = pencil.reshape(axial_total, -1)
    spectral = jnp.dot(axial_table.T, flat, precision=HIGHEST).reshape(pencil.shape)
    solved = radial_solve(spectral, axial_eig, theta_eig, radius_vec, angle_step)
    space = jnp.dot(axial_table, solved.reshape(axial_total, -1), precision=HIGHEST).reshape(
        pencil.shape
    )
    ahead = jnp.roll(space, -1, 0) - space
    back, back_step = (
        lax.all_to_all(space, "gz", split_axis=0, concat_axis=2, tiled=True),
        lax.all_to_all(ahead, "gz", split_axis=0, concat_axis=2, tiled=True),
    )
    pressure = to_space(back, around_table)
    axial_step = to_space(back_step, around_table)
    radial_step = (jnp.concatenate([pressure[:, 1:], pressure[:, -1:]], 1) - pressure) * open_radial
    around_step = (jnp.roll(pressure, -1, 2) - pressure) / (radii * angle_step) * open_around
    gradient = jnp.stack([radial_step, around_step, axial_step * open_axial])
    corrected = (predicted - DT_STEP * gradient).astype(jnp.bfloat16)[None]
    return (pressure, corrected)


MESH_ID = pl.DeviceIdType.MESH


def split_low(x):
    high = x.astype(jnp.bfloat16)
    return high, (x - high.astype(jnp.float32)).astype(jnp.bfloat16)


def triple_dot(x, table_high, table_low):
    high, low = split_low(x)
    out = jnp.dot(high, table_high, preferred_element_type=jnp.float32)
    out = out + jnp.dot(low, table_high, preferred_element_type=jnp.float32)
    return out + jnp.dot(high, table_low, preferred_element_type=jnp.float32)


def np_high_low(table):
    high = table.astype(jnp.bfloat16)
    low = (table - high.astype(np.float64)).astype(jnp.bfloat16)
    return high, low


@functools.lru_cache(maxsize=None)
def operator_tables(radial, around, axial, planes):
    half = around // 2
    rows = np.arange(around)[:, None]
    column = np.arange(around)[None, :]
    wave = np.where(column <= half, column, column - half)
    angle = 2.0 * np.pi / around * (rows * wave % around)
    basis = np.sqrt(2.0 / around) * np.where(column <= half, np.cos(angle), np.sin(angle))
    basis = np.where((column == 0) | (column == half), np.cos(angle) / np.sqrt(around), basis)
    radius = np.arange(radial) + 0.5
    inner = radius - 0.5
    outer = np.where(np.arange(radial) == radial - 1, 0.0, radius + 0.5)
    step = 2.0 * np.pi / around
    vectors, values = [], []
    for m in range(half + 1):
        eig = 2.0 - 2.0 * np.cos(2.0 * np.pi / around * m)
        matrix = np.diag((outer + inner) / radius + eig / (radius * step) ** 2)
        off = -outer[:-1] / np.sqrt(radius[:-1] * radius[1:])
        matrix = matrix + np.diag(off, 1) + np.diag(off, -1)
        value, vector = np.linalg.eigh(matrix)
        vector = vector * np.where(vector[:1] < 0.0, -1.0, 1.0)
        values.append(value)
        vectors.append(vector)
    vectors = np.stack(vectors, -1)
    values = np.maximum(np.stack(values, -1), 0.0)
    first = vectors[:, :, :half]
    nyquist = np.zeros((radial, max(radial, 128)))
    nyquist[:, :radial] = vectors[:, :, half].T
    other = np.concatenate([values[:, half:], values[:, 1:half]], -1)
    over = COMPRESS + np.stack([values[:, :half], other])
    root = np.sqrt(over * (over + 4.0))
    ratio = 2.0 / (2.0 + over + root)
    jump = ratio**planes
    wrap = 1.0 / (1.0 - ratio**axial)
    line = np.stack([ratio, 1.0 / root, jump, wrap], 1).astype(np.float32)
    ahead = np_high_low(basis)
    back = np_high_low(basis.T.copy())
    return (
        first.astype(np.float32),
        nyquist.astype(np.float32),
        line,
        np.stack(ahead),
        np.stack(back),
    )


def drum_kernel(
    gz_count,
    offsets_ref,
    diameters_ref,
    map_ref,
    wall_hbm,
    frac_hbm,
    velocity_hbm,
    gas_hbm,
    ahead_hbm,
    nyquist_hbm,
    line_hbm,
    back_hbm,
    radial_hbm,
    space_out,
    pred_out,
    fluid_out,
    wall_ref,
    frac_ref,
    velocity_ref,
    gas_ref,
    ahead_ref,
    nyquist_ref,
    line_ref,
    back_ref,
    fluid,
    pred,
    term,
    axial_flux,
    halo,
    modes,
    partner,
    radial,
    radial_back,
    lines,
    ends_out,
    ends_in,
    states_out,
    states_in,
    solved,
    result,
    space,
    table_sem,
    input_sem,
    out_sem,
    halo_sem,
    swap_send,
    swap_recv,
    ends_send,
    ends_recv,
    states_send,
    states_recv,
    back_send,
    back_recv,
):
    me = lax.axis_index("gz")
    ph = lax.axis_index("ph")
    other = 1 - ph
    planes, rows, around = term.shape
    half = around // 2
    axial_total = offsets_ref.shape[0]
    blocks = rows // 8
    angle_step = 2.0 * math.pi / around

    barrier = pltpu.get_barrier_semaphore()
    for hop in range(1, gz_count):
        pl.semaphore_signal(
            barrier, inc=1, device_id=(lax.rem(me + hop, gz_count), ph), device_id_type=MESH_ID
        )
    pl.semaphore_signal(barrier, inc=1, device_id=(me, other), device_id_type=MESH_ID)

    pairs = (
        (wall_hbm, wall_ref),
        (frac_hbm, frac_ref),
        (velocity_hbm, velocity_ref),
        (gas_hbm, gas_ref),
        (ahead_hbm, ahead_ref),
        (nyquist_hbm, nyquist_ref),
        (line_hbm, line_ref),
        (back_hbm, back_ref),
    )
    fetches = [pltpu.make_async_copy(a, b, input_sem.at[i]) for i, (a, b) in enumerate(pairs)]
    table_copy = pltpu.make_async_copy(radial_hbm, radial, table_sem)
    for fetch in fetches[:5]:
        fetch.start()
    table_copy.start()
    for fetch in fetches[5:]:
        fetch.start()
    fluid_copy = pltpu.make_async_copy(fluid, fluid_out, out_sem.at[0])
    pred_copy = pltpu.make_async_copy(pred, pred_out, out_sem.at[1])
    fetches[0].wait()

    radii = lax.broadcasted_iota(jnp.int32, (rows, around), 0).astype(jnp.float32) + 0.5
    row_id = lax.broadcasted_iota(jnp.int32, (rows, around), 0)
    wall = wall_ref[...].astype(jnp.float32).astype(jnp.bfloat16)
    from_col = lax.broadcasted_iota(jnp.int32, (around, around), 0)
    to_col = lax.broadcasted_iota(jnp.int32, (around, around), 1)
    gap = to_col - from_col

    def rotate(z, carry):
        turn = offsets_ref[lax.rem(me * planes + z, axial_total)]
        hit = (gap == turn) | (gap == turn - around)
        one_hot = jnp.where(hit, 1.0, 0.0).astype(jnp.bfloat16)
        fluid[z] = jnp.dot(wall, one_hot, preferred_element_type=jnp.float32)
        return carry

    lax.fori_loop(0, planes + 1, rotate, 0)

    fluid_copy.start()
    for fetch in fetches[1:4]:
        fetch.wait()
    size = diameters_ref[map_ref[0]]
    axial_flux[0] = jnp.zeros((rows, around), jnp.float32)

    def opens(z):
        here = fluid[z]
        open_radial = jnp.where(row_id == rows - 1, 0.0, here * pltpu.roll(here, rows - 1, 0))
        open_around = here * pltpu.roll(here, around - 1, 1)
        return open_radial, open_around, here * fluid[z + 1]

    weight = -jnp.sqrt(radii) / DT_STEP
    share = 1.0 / lax.axis_size("ph")

    def source(z, carry):
        volume = frac_ref[0, z].astype(jnp.float32)
        gas = [gas_ref[a, z].astype(jnp.float32) for a in range(3)]
        slip = [velocity_ref[0, a, z].astype(jnp.float32) - gas[a] for a in range(3)]
        speed = jnp.sqrt(1.0 + (slip[0] * slip[0] + slip[1] * slip[1] + slip[2] * slip[2]))
        beta = DRAG_SCALE * volume / (size * size) * (1.0 + 0.15 * speed)
        relax = 1.0 / (1.0 + DT_STEP * beta)
        open_radial, open_around, open_axial = opens(z)
        for a in range(3):
            pred[a, z] = gas[a] + relax * slip[a]
        pull = volume * relax
        flux_radial = (pull * slip[0] + share * gas[0]) * open_radial
        flux_around = (pull * slip[1] + share * gas[1]) * open_around
        flux_axial = (pull * slip[2] + share * gas[2]) * open_axial
        axial_flux[z + 1] = flux_axial
        out = (radii + 0.5) * flux_radial
        inward = jnp.where(row_id == 0, 0.0, pltpu.roll(out, 1, 0))
        total = (out - inward) / radii
        total = total + (flux_around - pltpu.roll(flux_around, 1, 1)) / (radii * angle_step)
        term[z] = (total + flux_axial - axial_flux[z]) * weight
        return carry

    lax.fori_loop(0, planes, source, 0)

    pred_copy.start()
    fetches[4].wait()
    pl.semaphore_wait(barrier, gz_count)

    halo_copy = pltpu.make_async_remote_copy(
        src_ref=axial_flux.at[planes],
        dst_ref=halo,
        send_sem=halo_sem.at[0],
        recv_sem=halo_sem.at[1],
        device_id=(lax.rem(me + 1, gz_count), ph),
        device_id_type=MESH_ID,
    )
    halo_copy.start()

    def swap(z):
        return pltpu.make_async_remote_copy(
            src_ref=modes.at[other, z],
            dst_ref=partner.at[z],
            send_sem=swap_send.at[z],
            recv_sem=swap_recv.at[z],
            device_id=(me, other),
            device_id_type=MESH_ID,
        )

    def to_modes(z, value):
        out = triple_dot(value, ahead_ref[0], ahead_ref[1])
        modes[0, z] = out[:, :half]
        modes[1, z] = out[:, half:]
        swap(z).start()

    def send_modes(k, carry):
        to_modes(k, term[k])
        return carry

    lax.fori_loop(1, planes, send_modes, 0)
    halo_copy.wait()
    to_modes(0, term[0] - halo[...] * weight)

    table_copy.wait()
    for fetch in fetches[5:]:
        fetch.wait()
    is_other = jnp.where(ph == 1, 1, 0)
    lane0 = (lax.broadcasted_iota(jnp.int32, (rows, half), 1) == 0) & (
        jnp.broadcast_to(is_other, (rows, half)) == 1
    )
    for r in range(rows):
        fill = jnp.broadcast_to(nyquist_ref[:, r : r + 1], (rows, half))
        radial[pl.ds(r * rows, rows), :] = jnp.where(lane0, fill, radial[pl.ds(r * rows, rows), :])

    def apply(table, load, z):
        def add(k, acc):
            for j in range(8):
                r = k * 8 + j
                line = jnp.broadcast_to(load(z, r), (rows, half))
                acc = acc + table[pl.ds(pl.multiple_of(r * rows, rows), rows), :] * line
            return acc

        return lax.fori_loop(0, rows // 8, add, jnp.zeros((rows, half), jnp.float32))

    def load_term(z, r):
        return modes[ph, z, pl.ds(r, 1), :] + partner[z, pl.ds(r, 1), :]

    def forward(k, carry):
        z = lax.rem(k + 1, planes)
        swap(z).wait_recv()
        lines[z] = apply(radial, load_term, z)
        return carry

    lax.fori_loop(0, planes, forward, 0)

    ratio = line_ref[ph, 0]
    rising = lines[0]
    for z in range(1, planes):
        rising = rising * ratio + lines[z]
    falling = lines[planes - 1]
    for z in range(planes - 2, -1, -1):
        falling = falling * ratio + lines[z]
    for j in range(blocks):
        ends_out[j] = rising[8 * j : 8 * j + 8]
        ends_out[blocks + j] = falling[8 * j : 8 * j + 8]

    def exchange(src, dst, send, recv, hop, sender):
        to = lax.rem(me + hop, gz_count)
        at = lax.rem(me + gz_count - hop, gz_count) if sender else me
        return pltpu.make_async_remote_copy(
            src_ref=src.at[to],
            dst_ref=dst.at[at],
            send_sem=send.at[hop],
            recv_sem=recv.at[hop],
            device_id=(to, ph),
            device_id_type=MESH_ID,
        )

    for hop in range(1, gz_count):
        exchange(ends_out, ends_in, ends_send, ends_recv, hop, False).start()
    ends_in[me] = ends_out[me]

    def flip(l, carry):
        radial_back[pl.ds(pl.multiple_of(l * rows, rows), rows), :] = radial[
            pl.ds(l, rows, stride=rows), :
        ]
        return carry

    lax.fori_loop(0, rows, flip, 0)

    for hop in range(1, gz_count):
        exchange(ends_out, ends_in, ends_send, ends_recv, hop, True).wait_recv()

    is_rise = 1 - me // blocks
    mine = lax.rem(me, blocks)
    jump = line_ref[ph, 2, pl.ds(pl.multiple_of(mine * 8, 8), 8), :]
    wrap = line_ref[ph, 3, pl.ds(pl.multiple_of(mine * 8, 8), 8), :]
    order = [is_rise * s + (1 - is_rise) * (gz_count - 1 - s) for s in range(gz_count)]
    state = jnp.zeros((8, half), jnp.float32)
    for s in range(gz_count):
        state = state * jump + ends_in[order[s]]
    state = state * wrap
    for s in range(gz_count):
        states_out[order[s]] = state
        state = state * jump + ends_in[order[s]]

    for hop in range(1, gz_count):
        exchange(states_out, states_in, states_send, states_recv, hop, False).start()
    states_in[me] = states_out[me]
    for hop in range(1, gz_count):
        exchange(states_out, states_in, states_send, states_recv, hop, True).wait_recv()

    scale = line_ref[ph, 1]
    right = jnp.concatenate([states_in[blocks + j] for j in range(blocks)], 0)
    left = jnp.concatenate([states_in[j] for j in range(blocks)], 0)
    solved[planes] = right
    behind = right * ratio
    for z in range(planes - 1, -1, -1):
        solved[z] = behind
        behind = (behind + lines[z]) * ratio
    ahead_state = left
    for z in range(planes):
        ahead_state = ahead_state * ratio + lines[z]
        solved[z] = (solved[z] + ahead_state) * scale
    solved[planes] = (solved[planes] + ahead_state * ratio) * scale

    def give(z, index):
        return pltpu.make_async_remote_copy(
            src_ref=result.at[index, z],
            dst_ref=result.at[index, z],
            send_sem=back_send.at[z],
            recv_sem=back_recv.at[z],
            device_id=(me, other),
            device_id_type=MESH_ID,
        )

    def load_solved(z, r):
        return solved[z, pl.ds(r, 1), :]

    shrink = 1.0 / jnp.sqrt(radii[:, :half])

    def inverse(z, carry):
        result[ph, z] = apply(radial_back, load_solved, z) * shrink
        give(z, ph).start()
        return carry

    lax.fori_loop(0, planes + 1, inverse, 0)

    def finish(z, carry):
        give(z, other).wait_recv()
        both = jnp.concatenate([result[0, z], result[1, z]], 1)
        space[z] = triple_dot(both, back_ref[0], back_ref[1])
        pltpu.make_async_copy(space.at[z], space_out.at[z], out_sem.at[z + 2]).start()
        return carry

    lax.fori_loop(0, planes + 1, finish, 0)

    for z in range(planes):
        swap(z).wait_send()
    for hop in range(1, gz_count):
        exchange(ends_out, ends_in, ends_send, ends_recv, hop, False).wait_send()
        exchange(states_out, states_in, states_send, states_recv, hop, False).wait_send()
    for z in range(planes + 1):
        give(z, ph).wait_send()
        pltpu.make_async_copy(space.at[z], space_out.at[z], out_sem.at[z + 2]).wait()
    fluid_copy.wait()
    pred_copy.wait()


def correct_kernel(space, space_next, pred, fluid, fluid_next, pressure_ref, corrected_ref):
    count, rows, around = space.shape
    radii = lax.broadcasted_iota(jnp.int32, (rows, around), 0).astype(jnp.float32) + 0.5
    row_id = lax.broadcasted_iota(jnp.int32, (rows, around), 0)
    angle_step = 2.0 * math.pi / around
    arc = 1.0 / (radii * angle_step)
    for z in range(count):
        here = space[z]
        mask = fluid[z]
        space_later = space[z + 1] if z + 1 < count else space_next[0]
        mask_later = fluid[z + 1] if z + 1 < count else fluid_next[0]
        pressure_ref[z] = here
        open_radial = jnp.where(row_id == rows - 1, 0.0, mask * pltpu.roll(mask, rows - 1, 0))
        open_around = mask * pltpu.roll(mask, around - 1, 1)
        radial_step = (pltpu.roll(here, rows - 1, 0) - here) * open_radial
        around_step = (pltpu.roll(here, around - 1, 1) - here) * arc * open_around
        axial_step = (space_later - here) * (mask * mask_later)
        for a, step in enumerate((radial_step, around_step, axial_step)):
            corrected_ref[0, a, z] = (pred[a, z] - DT_STEP * step).astype(jnp.bfloat16)


def drum_step(gz_count, frac, velocity, gas_vel, diameters, phase_map, wall_mask, offsets):
    planes, rows, around = frac.shape[1:]
    half = around // 2
    first, nyquist, line, ahead, back = operator_tables(rows, around, offsets.shape[0], planes)
    smem = pl.BlockSpec(memory_space=pltpu.SMEM)
    f32 = jnp.float32
    dma = pltpu.SemaphoreType.DMA
    ends = (gz_count, 8, half)
    space, pred, fluid = pl.pallas_call(
        functools.partial(drum_kernel, gz_count),
        out_shape=(
            jax.ShapeDtypeStruct((planes + 1, rows, around), f32),
            jax.ShapeDtypeStruct((3, planes, rows, around), f32),
            jax.ShapeDtypeStruct((planes + 1, rows, around), f32),
        ),
        in_specs=[smem] * 3 + [pl.BlockSpec(memory_space=pl.ANY)] * 9,
        out_specs=[pl.BlockSpec(memory_space=pl.ANY)] * 3,
        scratch_shapes=[
            pltpu.VMEM(wall_mask.shape, jnp.int32),
            pltpu.VMEM(frac.shape, jnp.bfloat16),
            pltpu.VMEM(velocity.shape, jnp.bfloat16),
            pltpu.VMEM(gas_vel.shape, jnp.bfloat16),
            pltpu.VMEM(ahead.shape, jnp.bfloat16),
            pltpu.VMEM(nyquist.shape, f32),
            pltpu.VMEM(line.shape, f32),
            pltpu.VMEM(back.shape, jnp.bfloat16),
            pltpu.VMEM((planes + 1, rows, around), f32),
            pltpu.VMEM((3, planes, rows, around), f32),
            pltpu.VMEM((planes, rows, around), f32),
            pltpu.VMEM((planes + 1, rows, around), f32),
            pltpu.VMEM((rows, around), f32),
            pltpu.VMEM((2, planes, rows, half), f32),
            pltpu.VMEM((planes, rows, half), f32),
            pltpu.VMEM((rows * rows, half), f32),
            pltpu.VMEM((rows * rows, half), f32),
            pltpu.VMEM((planes, rows, half), f32),
            pltpu.VMEM(ends, f32),
            pltpu.VMEM(ends, f32),
            pltpu.VMEM(ends, f32),
            pltpu.VMEM(ends, f32),
            pltpu.VMEM((planes + 1, rows, half), f32),
            pltpu.VMEM((2, planes + 1, rows, half), f32),
            pltpu.VMEM((planes + 1, rows, around), f32),
            dma,
            dma((8,)),
            dma((planes + 3,)),
            dma((2,)),
            dma((planes,)),
            dma((planes,)),
            dma((gz_count,)),
            dma((gz_count,)),
            dma((gz_count,)),
            dma((gz_count,)),
            dma((planes + 1,)),
            dma((planes + 1,)),
        ],
        compiler_params=pltpu.CompilerParams(
            collective_id=0, has_side_effects=True, vmem_limit_bytes=56 * 1024 * 1024
        ),
    )(
        offsets,
        diameters,
        phase_map,
        wall_mask,
        frac,
        velocity,
        gas_vel,
        jnp.asarray(ahead),
        jnp.asarray(nyquist),
        jnp.asarray(line),
        jnp.asarray(back),
        jnp.asarray(first.reshape(rows * rows, half)),
    )
    chunk = planes // CORRECT_STEPS if planes % CORRECT_STEPS == 0 else planes
    here = pl.BlockSpec((chunk, rows, around), lambda k: (k, 0, 0))
    later = pl.BlockSpec((1, rows, around), lambda k: ((k + 1) * chunk, 0, 0))
    return pl.pallas_call(
        correct_kernel,
        grid=(planes // chunk,),
        out_shape=(
            jax.ShapeDtypeStruct((planes, rows, around), f32),
            jax.ShapeDtypeStruct((1, 3, planes, rows, around), jnp.bfloat16),
        ),
        in_specs=[
            here,
            later,
            pl.BlockSpec((3, chunk, rows, around), lambda k: (0, k, 0, 0)),
            here,
            later,
        ],
        out_specs=(here, pl.BlockSpec((1, 3, chunk, rows, around), lambda k: (0, 0, k, 0, 0))),
    )(space, space, pred, fluid, fluid)


def solution(mesh):
    in_specs = (
        P("ph", "gz", None, None),
        P("ph", None, "gz", None, None),
        P(None, "gz", None, None),
        P(),
        P("ph"),
        P(),
        P(),
    )
    out_specs = (P("gz", None, None), P("ph", None, "gz", None, None))
    gz_count, ph_count = mesh.shape["gz"], mesh.shape["ph"]

    def body(frac, *rest):
        rows, around = frac.shape[2:]
        fits = ph_count == 2 and around == 256 and rows <= 128
        if fits and rows * 2 == gz_count * 8 and frac.shape[1] <= 8:
            return drum_step(gz_count, frac, *rest)
        return shards(frac, *rest)

    return jax.shard_map(body, mesh=mesh, in_specs=in_specs, out_specs=out_specs, check_vma=False)
```
